32 devices in a mesh: freq: 8 (over z, core), tile: 4 (over y, x).
Axes of the slice: x: 2, y: 2, z: 4, core: 2. Of those that a mesh axis runs over, the one named last changes fastest.
Arguments:
- wave: float32 [2, 2, 8, 256, 1024], P(None, None, 'freq', 'tile'), may hold values from -6 to 6
- velocity: float32 [3, 256, 1024], P(None, 'tile'), may hold values from 1500 to 4500
Outputs:
- image: float32 [3, 16, 256, 1024], P(None, 'freq', 'tile')
The draws below stay inside these ranges and needn't reach their ends.
All inputs are finite; a program needn't handle non-finite values.
Results may differ from the reference program's by a relative error of at most 0.0001.
Values sent between devices are 32-bit elements; how exact they have to be, the bound alone decides.
A program may use at most 128 MiB of HBM per device.

```python
import math
import jax
import jax.numpy as jnp
from jax import lax

NY = 1024
STEPS = 3
SWEEPS = 8
OFFS = 16
FREQS = 8
NX = 256


def block_scale(stream_key, dims, pieces, least, high):
    def one(dim, blocks):
        draws = jax.random.uniform(jax.random.fold_in(jax.random.fold_in(stream_key, 6), dim), (blocks,), jnp.float32, least / len(pieces), high / len(pieces))
        return jnp.repeat(jnp.exp(draws), dims[dim] // blocks).reshape((-1,) + (1,) * (len(dims) - dim - 1))

    factor_of = one(*pieces[0])
    for cut in pieces[1:]:
        factor_of = factor_of * one(*cut)
    return factor_of


def bell_draw(own_key, extent, scale, most, shards=(), kind=jnp.bfloat16):
    values = scale * jax.random.normal(own_key, extent, jnp.float32)
    if shards:
        values = values * block_scale(own_key, extent, shards, -0.22, 0.18)
    return jnp.clip(values, -most, most).astype(kind)


def setup_inputs(seed: int = 0) -> dict:
    key_of = jax.random.split(jax.random.key(seed), 3)
    wave = bell_draw(key_of[0], (2, 2, FREQS, NX, NY), 1.0, 6.0, ((2, 8), (3, 4)), jnp.float32)
    velocity = jnp.clip(jnp.exp(math.log(4500.0) - 1.0986123 * jax.random.uniform(key_of[1], (STEPS, NX, NY), jnp.float32) ** block_scale(key_of[1], (STEPS, NX, NY), ((1, 4),), -0.2, 0.2)), 1500.0, 4500.0)
    return {"wave": wave, "velocity": velocity}


pade_first = 0.376393
pade_second = 0.478242
layer_thickness = 10.0
grid_spacing = 15.0
full_turn = 2.0 * math.pi

def stencil(padded):
    edges = padded[..., 2:, 1:-1] + padded[..., :-2, 1:-1] + padded[..., 1:-1, 2:] + padded[..., 1:-1, :-2]
    corners = padded[..., 2:, 2:] + padded[..., 2:, :-2] + padded[..., :-2, 2:] + padded[..., :-2, :-2]
    return 4.0 * edges + corners

def pad_both(field):
    return jnp.pad(field, [(0, 0)] * (field.ndim - 2) + [(1, 1), (1, 1)])

def coefficients(speeds, angular, parity):
    speed_grid = speeds[None, None]
    angular_col = angular[None, :, None, None]
    parity_col = parity[:, None, None, None]
    real_coef = pade_second * (speed_grid / (angular_col * grid_spacing)) ** 2
    imag_coef = -parity_col * pade_first * layer_thickness * speed_grid / (2.0 * angular_col * grid_spacing ** 2)
    return (real_coef, imag_coef)

def phase_screen(fields, speeds, angular, parity):
    phase_angle = parity[:, None, None, None] * angular[None, :, None, None] * layer_thickness / speeds[None, None]
    cosine = jnp.cos(phase_angle)
    sine_part = jnp.sin(phase_angle)
    wave_real = fields[:, 0] * cosine + fields[:, 1] * sine_part
    wave_imag = fields[:, 1] * cosine - fields[:, 0] * sine_part
    return jnp.stack([wave_real, wave_imag], axis=1)

def operator_terms(screened, nearby, real_coef, imag_coef):
    laplace = (nearby - 20.0 * screened) / 6.0
    rhs_real = screened[:, 0] - (real_coef * laplace[:, 0] + imag_coef * laplace[:, 1])
    rhs_imag = screened[:, 1] - (real_coef * laplace[:, 1] - imag_coef * laplace[:, 0])
    diagonal = 6.0 + 20.0 * real_coef
    denominator = diagonal * diagonal + 400.0 * imag_coef * imag_coef
    couple_real = (real_coef * diagonal + 20.0 * imag_coef * imag_coef) / denominator
    couple_imag = 6.0 * imag_coef / denominator
    base_real = 6.0 * (rhs_real * diagonal + 20.0 * imag_coef * rhs_imag) / denominator
    base_imag = 6.0 * (rhs_imag * diagonal - 20.0 * imag_coef * rhs_real) / denominator
    return (base_real, base_imag, couple_real, couple_imag)

def jacobi_update(nearby, terms):
    base_real, base_imag, couple_real, couple_imag = terms
    new_real = base_real + couple_real * nearby[:, 0] - couple_imag * nearby[:, 1]
    new_imag = base_imag + couple_real * nearby[:, 1] + couple_imag * nearby[:, 0]
    return jnp.stack([new_real, new_imag], axis=1)

def image_terms(fields, offsets, width):
    half_offs = offsets // 2
    padded = jnp.pad(fields, [(0, 0)] * 4 + [(half_offs, half_offs)])
    image_rows = []
    for offset in range(offsets):
        source = padded[0, :, :, :, 2 * half_offs - offset:2 * half_offs - offset + width]
        receiver = padded[1, :, :, :, offset:offset + width]
        image_rows.append(lax.optimization_barrier(jnp.sum(source[0] * receiver[0] + source[1] * receiver[1], axis=0)))
    return jnp.stack(image_rows)

def reference(wave, velocity):
    freq_index = jnp.arange(FREQS, dtype=jnp.float32)
    angular = full_turn * (8.0 + 48.0 * freq_index / FREQS)
    parity = jnp.array([1.0, -1.0], dtype=jnp.float32)
    fields = wave
    images = []
    for depth_level in range(STEPS):
        screened = phase_screen(fields, velocity[depth_level], angular, parity)
        real_coef, imag_coef = coefficients(velocity[depth_level], angular, parity)
        terms = operator_terms(screened, stencil(pad_both(screened)), real_coef, imag_coef)
        current = screened
        for sweep_count in range(SWEEPS):
            current = jacobi_update(stencil(pad_both(current)), terms)
        fields = current
        images.append(image_terms(fields, OFFS, NY) * (1.0 / math.sqrt(FREQS)))
    return jnp.stack(images)
```

```python
import functools
import math

import jax
import jax.numpy as jnp
from jax import lax
from jax.experimental import pallas as pl
from jax.experimental.pallas import tpu as pltpu
from jax.sharding import PartitionSpec as P

STEPS = 3
SWEEPS = 8
OFFS = 16
HALO = 8
LANES = 128

pade_first = 0.376393
pade_second = 0.478242
layer_thickness = 10.0
grid_spacing = 15.0
full_turn = 2.0 * math.pi
angle_mid = 1.2
MESH = pl.DeviceIdType.MESH


def cos_sin(angle):
    y = angle - angle_mid
    z = y * y
    sine = -1.0 / math.factorial(11)
    for power in (9, 7, 5, 3, 1):
        sine = sine * z + (-1.0) ** (power // 2) / math.factorial(power)
    sine = sine * y
    cosine = 1.0 / math.factorial(12)
    for power in (10, 8, 6, 4, 2, 0):
        cosine = cosine * z + (-1.0) ** (power // 2) / math.factorial(power)
    mid_cos, mid_sin = math.cos(angle_mid), math.sin(angle_mid)
    return cosine * mid_cos - sine * mid_sin, sine * mid_cos + cosine * mid_sin


def kernel(
    n, tiles, group, wave_ref, velocity_ref, out_ref, nat, halo, vel, cur, base, coup, recv, img, part,
    vel_sems, halo_sems, field_send, field_recv, image_send, image_recv,
):
    rows, width = velocity_ref.shape[1:]
    cols = width // LANES
    ext = rows + 2 * HALO
    count = ext // 8
    chunk = rows // group
    groups = n // group
    per_dev = OFFS // n
    me = lax.axis_index("freq")
    tile = lax.axis_index("tile")
    my_group, member = me // group, me % group
    has_up, has_down = tile > 0, tile < tiles - 1

    lane = lax.broadcasted_iota(jnp.int32, (8, LANES), 1)
    sub = lax.broadcasted_iota(jnp.int32, (8, LANES), 0)
    angular = full_turn * (8.0 + 48.0 * jnp.full((8, LANES), me, jnp.int32).astype(jnp.float32) / n)
    zero = jnp.zeros((8, LANES), jnp.float32)

    def strided(i):
        return pl.ds(i, 8, stride=count)

    def row_valid(i):
        row = sub * count + (i - HALO + tile * rows)
        return (row >= 0) & (row < tiles * rows)

    def stage(k, _):
        top = pl.multiple_of(k * 8, 8)
        for j in range(cols):
            at = pl.ds(j * LANES, LANES)
            for c in range(4):
                nat[0, c, j, pl.ds(top + HALO, 8), :] = wave_ref[c // 2, c % 2, 0, pl.ds(top, 8), at]
            for d in range(STEPS):
                vel[d, j, pl.ds(top + HALO, 8), :] = velocity_ref[d, pl.ds(top, 8), at]
        return 0

    lax.fori_loop(0, rows // 8, stage, 0)

    barrier = pltpu.get_barrier_semaphore()
    for k in range(1, n):
        pl.semaphore_signal(barrier, inc=1, device_id={"freq": (me + k) % n}, device_id_type=MESH)

    @pl.when(has_up)
    def _():
        pl.semaphore_signal(barrier, inc=1, device_id={"tile": tile - 1}, device_id_type=MESH)

    @pl.when(has_down)
    def _():
        pl.semaphore_signal(barrier, inc=1, device_id={"tile": tile + 1}, device_id_type=MESH)

    near = (tile + tiles - 1) // tiles + (2 * tiles - 2 - tile) // tiles
    pl.semaphore_wait(barrier, n - 1 + near)

    def halo_copy(d, side):
        start = HALO if side == 0 else rows
        return pltpu.make_async_remote_copy(
            src_ref=nat.at[d, :, :, pl.ds(start, HALO), :],
            dst_ref=halo.at[d, side],
            send_sem=halo_sems.at[0, d, side],
            recv_sem=halo_sems.at[1, d, side],
            device_id={"tile": tile - 1 if side == 0 else tile + 1},
            device_id_type=MESH,
        )

    def vel_copy(side):
        start = HALO if side == 0 else rows
        land = rows + HALO if side == 0 else 0
        return pltpu.make_async_remote_copy(
            src_ref=vel.at[:, :, pl.ds(start, HALO), :],
            dst_ref=vel.at[:, :, pl.ds(land, HALO), :],
            send_sem=vel_sems.at[0, side],
            recv_sem=vel_sems.at[1, side],
            device_id={"tile": tile - 1 if side == 0 else tile + 1},
            device_id_type=MESH,
        )

    def field_copy(d, k, sender):
        peer = (member + k) % group
        return pltpu.make_async_remote_copy(
            src_ref=nat.at[d + 1, :, :, pl.ds(pl.multiple_of(HALO + peer * chunk, 8), chunk), :],
            dst_ref=recv.at[d, sender],
            send_sem=field_send.at[d, k],
            recv_sem=field_recv.at[d, sender],
            device_id={"freq": my_group * group + peer},
            device_id_type=MESH,
        )

    def image_copy(d, k, sender):
        peer = (me + k) % n
        top = pl.multiple_of((sender % group) * chunk, 8)
        return pltpu.make_async_remote_copy(
            src_ref=img.at[d, pl.ds(peer * per_dev, per_dev)],
            dst_ref=part.at[d, sender // group, :, pl.ds(top, chunk), :],
            send_sem=image_send.at[d, k],
            recv_sem=image_recv.at[d, sender],
            device_id={"freq": peer},
            device_id_type=MESH,
        )

    def send_halos(d):
        @pl.when(has_up)
        def _():
            halo_copy(d, 0).start()

        @pl.when(has_down)
        def _():
            halo_copy(d, 1).start()

    def take_halos(d):
        @pl.when(has_up)
        def _():
            halo_copy(d, 1).wait_recv()
            for c in range(4):
                for j in range(cols):
                    nat[d, c, j, 0:HALO, :] = halo[d, 1, c, j]

        @pl.when(has_down)
        def _():
            halo_copy(d, 0).wait_recv()
            for c in range(4):
                for j in range(cols):
                    nat[d, c, j, rows + HALO : rows + 2 * HALO, :] = halo[d, 0, c, j]

    @pl.when(has_up)
    def _():
        vel_copy(0).start()

    @pl.when(has_down)
    def _():
        vel_copy(1).start()

    send_halos(0)

    @pl.when(has_up)
    def _():
        vel_copy(1).wait_recv()

    @pl.when(has_down)
    def _():
        vel_copy(0).wait_recv()

    def wrap_rows(slot):
        for c in range(4):
            for j in range(cols):
                cur[slot, c, 0, j] = pltpu.roll(cur[slot, c, count, j], 1, 0)
                cur[slot, c, count + 1, j] = pltpu.roll(cur[slot, c, 1, j], 7, 0)

    def quarter_stencil(slot, c, i):
        sums, to_right, to_left = [], [], []
        for j in range(cols):
            pair = cur[slot, c, i, j] + cur[slot, c, i + 2, j]
            mixed = cur[slot, c, i + 1, j] + 0.25 * pair
            sums.append(pair)
            to_right.append(pltpu.roll(mixed, 1, 1))
            to_left.append(pltpu.roll(mixed, LANES - 1, 1))
        out = []
        for j in range(cols):
            left = jnp.where(lane == 0, to_right[j - 1] if j else zero, to_right[j])
            right = jnp.where(lane == LANES - 1, to_left[j + 1] if j < cols - 1 else zero, to_left[j])
            out.append(sums[j] + (left + right))
        return out

    def depth_step(d):
        take_halos(d)

        def screen(i, _):
            valid = row_valid(i)
            for j in range(cols):
                cosine, sine = cos_sin(angular * layer_thickness / vel[d, j, strided(i), :])
                sr, si, rr, ri = [nat[d, c, j, strided(i), :] for c in range(4)]
                cur[0, 0, i + 1, j] = jnp.where(valid, sr * cosine + si * sine, 0.0)
                cur[0, 1, i + 1, j] = jnp.where(valid, si * cosine - sr * sine, 0.0)
                cur[0, 2, i + 1, j] = jnp.where(valid, rr * cosine - ri * sine, 0.0)
                cur[0, 3, i + 1, j] = jnp.where(valid, ri * cosine + rr * sine, 0.0)
            return 0

        lax.fori_loop(0, count, screen, 0)
        wrap_rows(0)

        def first(i, _):
            valid = row_valid(i)
            for field in range(2):
                near_r = quarter_stencil(0, 2 * field, i)
                near_i = quarter_stencil(0, 2 * field + 1, i)
                for j in range(cols):
                    speed = vel[d, j, strided(i), :]
                    real = pade_second * (speed / (angular * grid_spacing)) ** 2
                    imag = -pade_first * layer_thickness * speed / (2.0 * angular * grid_spacing**2)
                    if field:
                        imag = -imag
                    diag = 6.0 + 20.0 * real
                    inverse = 1.0 / (diag * diag + 400.0 * imag * imag)
                    couple_r = jnp.where(valid, 4.0 * (real * diag + 20.0 * imag * imag) * inverse, 0.0)
                    couple_i = jnp.where(valid, 24.0 * imag * inverse, 0.0)
                    u_r, u_i = cur[0, 2 * field, i + 1, j], cur[0, 2 * field + 1, i + 1, j]
                    lap_r = (4.0 * near_r[j] - 20.0 * u_r) * (1.0 / 6.0)
                    lap_i = (4.0 * near_i[j] - 20.0 * u_i) * (1.0 / 6.0)
                    rhs_r = u_r - (real * lap_r + imag * lap_i)
                    rhs_i = u_i - (real * lap_i - imag * lap_r)
                    base_r = jnp.where(valid, 6.0 * (rhs_r * diag + 20.0 * imag * rhs_i) * inverse, 0.0)
                    base_i = jnp.where(valid, 6.0 * (rhs_i * diag - 20.0 * imag * rhs_r) * inverse, 0.0)
                    base[2 * field, i, j] = base_r
                    base[2 * field + 1, i, j] = base_i
                    if not field:
                        coup[0, i, j] = couple_r
                        coup[1, i, j] = couple_i
                    cur[1, 2 * field, i + 1, j] = base_r + (couple_r * near_r[j] - couple_i * near_i[j])
                    cur[1, 2 * field + 1, i + 1, j] = base_i + (couple_r * near_i[j] + couple_i * near_r[j])
            return 0

        lax.fori_loop(0, count, first, 0)
        wrap_rows(1)

        def update(slot, i, store):
            for field in range(2):
                near_r = quarter_stencil(slot, 2 * field, i)
                near_i = quarter_stencil(slot, 2 * field + 1, i)
                for j in range(cols):
                    couple_r, couple_i = coup[0, i, j], coup[1, i, j]
                    base_r, base_i = base[2 * field, i, j], base[2 * field + 1, i, j]
                    cross_r, cross_i = couple_i * near_i[j], couple_i * near_r[j]
                    if field:
                        store(2, i, j, base_r + couple_r * near_r[j] + cross_r)
                        store(3, i, j, base_i + couple_r * near_i[j] - cross_i)
                    else:
                        store(0, i, j, base_r + couple_r * near_r[j] - cross_r)
                        store(1, i, j, base_i + couple_r * near_i[j] + cross_i)

        def sweep(s, _):
            slot = s % 2

            def store(c, i, j, value):
                cur[1 - slot, c, i + 1, j] = value

            def body(i, _):
                update(slot, i, store)
                return 0

            lax.fori_loop(0, count, body, 0)
            wrap_rows(1 - slot)
            return 0

        lax.fori_loop(1, SWEEPS - 1, sweep, 0)

        def store_last(c, i, j, value):
            nat[d + 1, c, j, strided(i), :] = value

        def last(i, _):
            update((SWEEPS - 1) % 2, i, store_last)
            return 0

        lax.fori_loop(0, count, last, 0)

        @pl.when(d + 1 < STEPS)
        def _():
            send_halos(d + 1)

        for k in range(1, group):
            field_copy(d, k, member).start()
        top = pl.multiple_of(HALO + member * chunk, 8)

        def keep(c, _):
            recv[d, member, c] = nat[d + 1, c, :, pl.ds(top, chunk), :]
            return 0

        lax.fori_loop(0, 4, keep, 0)

    def shifted(blocks, move):
        if move == 0:
            return blocks
        if move > 0:
            rolled = [pltpu.roll(b, LANES - move, 1) for b in blocks] + [zero]
            inside = lane < LANES - move
            return [jnp.where(inside, rolled[j], rolled[j + 1]) for j in range(cols)]
        rolled = [zero] + [pltpu.roll(b, -move, 1) for b in blocks]
        inside = lane >= -move
        return [jnp.where(inside, rolled[j + 1], rolled[j]) for j in range(cols)]

    def image_step(d):
        for k in range(1, group):
            field_copy(d, k, (member + k) % group).wait_recv()

        def block(rb, _):
            top = pl.multiple_of(rb * 8, 8)
            for o in range(OFFS):
                h = o - OFFS // 2

                def add(q, acc):
                    real = shifted([recv[d, q, 2, j, pl.ds(top, 8), :] for j in range(cols)], 2 * h)
                    imag = shifted([recv[d, q, 3, j, pl.ds(top, 8), :] for j in range(cols)], 2 * h)
                    return tuple(
                        acc[j]
                        + (recv[d, q, 0, j, pl.ds(top, 8), :] * real[j] + recv[d, q, 1, j, pl.ds(top, 8), :] * imag[j])
                        for j in range(cols)
                    )

                total = shifted(list(lax.fori_loop(0, group, add, (zero,) * cols)), -h)
                for j in range(cols):
                    img[d, o, pl.ds(top, 8), pl.ds(j * LANES, LANES)] = total[j] * (1.0 / math.sqrt(n))
            return 0

        lax.fori_loop(0, chunk // 8, block, 0)
        for k in range(1, n):
            image_copy(d, k, me).start()
        place = pl.multiple_of(member * chunk, 8)
        for o in range(per_dev):
            part[d, my_group, o, pl.ds(place, chunk), :] = img[d, me * per_dev + o]

    def pipeline(d, _):
        @pl.when(d < STEPS)
        def _():
            depth_step(d)

        @pl.when(d > 0)
        def _():
            image_step(d - 1)

        return 0

    lax.fori_loop(0, STEPS + 1, pipeline, 0)

    def finish(d, _):
        for k in range(1, n):
            image_copy(d, k, (me + k) % n).wait_recv()

        def merge(b, _):
            top = pl.multiple_of(b * 8, 8)
            for o in range(per_dev):
                total = part[d, 0, o, pl.ds(top, 8), :]
                for gr in range(1, groups):
                    total = total + part[d, gr, o, pl.ds(top, 8), :]
                out_ref[d, o, pl.ds(top, 8), :] = total
            return 0

        lax.fori_loop(0, rows // 8, merge, 0)
        for k in range(1, group):
            field_copy(d, k, member).wait_send()
        for k in range(1, n):
            image_copy(d, k, me).wait_send()

        @pl.when(has_up)
        def _():
            halo_copy(d, 0).wait_send()

        @pl.when(has_down)
        def _():
            halo_copy(d, 1).wait_send()

        return 0

    lax.fori_loop(0, STEPS, finish, 0)

    @pl.when(has_up)
    def _():
        vel_copy(0).wait_send()

    @pl.when(has_down)
    def _():
        vel_copy(1).wait_send()


def on_device(n, tiles, wave, velocity):
    rows, width = velocity.shape[1:]
    cols = width // LANES
    ext = rows + 2 * HALO
    count = ext // 8
    group = min(4, n)
    chunk = rows // group
    per_dev = OFFS // n
    f32 = jnp.float32
    dma = pltpu.SemaphoreType.DMA
    return pl.pallas_call(
        functools.partial(kernel, n, tiles, group),
        out_shape=jax.ShapeDtypeStruct((STEPS, per_dev, rows, width), f32),
        in_specs=[pl.BlockSpec(memory_space=pltpu.VMEM)] * 2,
        out_specs=pl.BlockSpec(memory_space=pltpu.VMEM),
        scratch_shapes=[
            pltpu.VMEM((STEPS + 1, 4, cols, ext, LANES), f32),
            pltpu.VMEM((STEPS, 2, 4, cols, HALO, LANES), f32),
            pltpu.VMEM((STEPS, cols, ext, LANES), f32),
            pltpu.VMEM((2, 4, count + 2, cols, 8, LANES), f32),
            pltpu.VMEM((4, count, cols, 8, LANES), f32),
            pltpu.VMEM((2, count, cols, 8, LANES), f32),
            pltpu.VMEM((STEPS, group, 4, cols, chunk, LANES), f32),
            pltpu.VMEM((STEPS, OFFS, chunk, width), f32),
            pltpu.VMEM((STEPS, n // group, per_dev, rows, width), f32),
            dma((2, 2)),
            dma((2, STEPS, 2)),
            dma((STEPS, group)),
            dma((STEPS, group)),
            dma((STEPS, n)),
            dma((STEPS, n)),
        ],
        compiler_params=pltpu.CompilerParams(
            collective_id=0, has_side_effects=True, vmem_limit_bytes=56 * 2**20
        ),
        name="migrate",
    )(wave, velocity)


def solution(mesh):
    placed = (P(None, None, "freq", "tile", None), P(None, "tile", None))
    return jax.shard_map(
        functools.partial(on_device, mesh.shape["freq"], mesh.shape["tile"]),
        mesh=mesh,
        in_specs=placed,
        out_specs=P(None, "freq", "tile", None),
        check_vma=False,
    )
```

```python
import functools
import math

import jax
import jax.numpy as jnp
from jax import lax
from jax.experimental import pallas as pl
from jax.experimental.pallas import tpu as pltpu
from jax.sharding import PartitionSpec as P

STEPS = 3
SWEEPS = 8
OFFS = 16
HALO = 8
LANES = 128
BATCH = 2

pade_first = 0.376393
pade_second = 0.478242
layer_thickness = 10.0
grid_spacing = 15.0
full_turn = 2.0 * math.pi
angle_mid = 1.2
MESH = pl.DeviceIdType.MESH


def cos_sin(angle):
    y = angle - angle_mid
    z = y * y
    sine = -1.0 / math.factorial(11)
    for power in (9, 7, 5, 3, 1):
        sine = sine * z + (-1.0) ** (power // 2) / math.factorial(power)
    sine = sine * y
    cosine = 1.0 / math.factorial(12)
    for power in (10, 8, 6, 4, 2, 0):
        cosine = cosine * z + (-1.0) ** (power // 2) / math.factorial(power)
    mid_cos, mid_sin = math.cos(angle_mid), math.sin(angle_mid)
    return cosine * mid_cos - sine * mid_sin, sine * mid_cos + cosine * mid_sin


def kernel(
    n, tiles, group, wave_ref, velocity_ref, out_ref, nat, halo, vel, cur_a, cur_b, base, coup, recv, img, part,
    vel_sems, halo_sems, field_send, field_recv, image_send, image_recv,
):
    rows, width = velocity_ref.shape[1:]
    cols = width // LANES
    ext = rows + 2 * HALO
    count = ext // 8
    chunk = rows // group
    groups = n // group
    per_dev = OFFS // n
    me = lax.axis_index("freq")
    tile = lax.axis_index("tile")
    my_group, member = me // group, me % group
    has_up, has_down = tile > 0, tile < tiles - 1

    lane = lax.broadcasted_iota(jnp.int32, (8, LANES), 1)
    sub = lax.broadcasted_iota(jnp.int32, (8, LANES), 0)
    angular = full_turn * (8.0 + 48.0 * jnp.full((8, LANES), me, jnp.int32).astype(jnp.float32) / n)
    zero = jnp.zeros((8, LANES), jnp.float32)

    def strided(i):
        return pl.ds(i, 8, stride=count)

    def row_valid(i):
        row = sub * count + (i - HALO + tile * rows)
        return (row >= 0) & (row < tiles * rows)

    def stage(k, _):
        top = pl.multiple_of(k * 8, 8)
        for j in range(cols):
            at = pl.ds(j * LANES, LANES)
            for c in range(4):
                nat[0, c, j, pl.ds(top + HALO, 8), :] = wave_ref[c // 2, c % 2, 0, pl.ds(top, 8), at]
            for d in range(STEPS):
                vel[d, j, pl.ds(top + HALO, 8), :] = velocity_ref[d, pl.ds(top, 8), at]
        return 0

    lax.fori_loop(0, rows // 8, stage, 0)

    barrier = pltpu.get_barrier_semaphore()
    for k in range(1, n):
        pl.semaphore_signal(barrier, inc=1, device_id={"freq": (me + k) % n}, device_id_type=MESH)

    @pl.when(has_up)
    def _():
        pl.semaphore_signal(barrier, inc=1, device_id={"tile": tile - 1}, device_id_type=MESH)

    @pl.when(has_down)
    def _():
        pl.semaphore_signal(barrier, inc=1, device_id={"tile": tile + 1}, device_id_type=MESH)

    near = (tile + tiles - 1) // tiles + (2 * tiles - 2 - tile) // tiles
    pl.semaphore_wait(barrier, n - 1 + near)

    def halo_copy(d, side):
        start = HALO if side == 0 else rows
        return pltpu.make_async_remote_copy(
            src_ref=nat.at[d, :, :, pl.ds(start, HALO), :],
            dst_ref=halo.at[d, side],
            send_sem=halo_sems.at[0, d, side],
            recv_sem=halo_sems.at[1, d, side],
            device_id={"tile": tile - 1 if side == 0 else tile + 1},
            device_id_type=MESH,
        )

    def vel_copy(side):
        start = HALO if side == 0 else rows
        land = rows + HALO if side == 0 else 0
        return pltpu.make_async_remote_copy(
            src_ref=vel.at[:, :, pl.ds(start, HALO), :],
            dst_ref=vel.at[:, :, pl.ds(land, HALO), :],
            send_sem=vel_sems.at[0, side],
            recv_sem=vel_sems.at[1, side],
            device_id={"tile": tile - 1 if side == 0 else tile + 1},
            device_id_type=MESH,
        )

    def field_copy(d, k, sender):
        peer = (member + k) % group
        return pltpu.make_async_remote_copy(
            src_ref=nat.at[d + 1, :, :, pl.ds(pl.multiple_of(HALO + peer * chunk, 8), chunk), :],
            dst_ref=recv.at[d, sender],
            send_sem=field_send.at[d, k],
            recv_sem=field_recv.at[d, sender],
            device_id={"freq": my_group * group + peer},
            device_id_type=MESH,
        )

    def image_copy(d, k, sender):
        peer = (me + k) % n
        top = pl.multiple_of((sender % group) * chunk, 8)
        return pltpu.make_async_remote_copy(
            src_ref=img.at[d, pl.ds(peer * per_dev, per_dev)],
            dst_ref=part.at[d, sender // group, :, pl.ds(top, chunk), :],
            send_sem=image_send.at[d, k],
            recv_sem=image_recv.at[d, sender],
            device_id={"freq": peer},
            device_id_type=MESH,
        )

    def send_halos(d):
        @pl.when(has_up)
        def _():
            halo_copy(d, 0).start()

        @pl.when(has_down)
        def _():
            halo_copy(d, 1).start()

    def take_halos(d):
        @pl.when(has_up)
        def _():
            halo_copy(d, 1).wait_recv()
            for c in range(4):
                for j in range(cols):
                    nat[d, c, j, 0:HALO, :] = halo[d, 1, c, j]

        @pl.when(has_down)
        def _():
            halo_copy(d, 0).wait_recv()
            for c in range(4):
                for j in range(cols):
                    nat[d, c, j, rows + HALO : rows + 2 * HALO, :] = halo[d, 0, c, j]

    @pl.when(has_up)
    def _():
        vel_copy(0).start()

    @pl.when(has_down)
    def _():
        vel_copy(1).start()

    send_halos(0)

    @pl.when(has_up)
    def _():
        vel_copy(1).wait_recv()

    @pl.when(has_down)
    def _():
        vel_copy(0).wait_recv()

    def wrap_rows(ref):
        for c in range(4):
            for j in range(cols):
                ref[c, 0, j] = pltpu.roll(ref[c, count, j], 1, 0)
                ref[c, count + 1, j] = pltpu.roll(ref[c, 1, j], 7, 0)

    def quarter_stencil(above, here, below):
        sums, to_right, to_left = [], [], []
        for j in range(cols):
            pair = above[j] + below[j]
            mixed = here[j] + 0.25 * pair
            sums.append(pair)
            to_right.append(pltpu.roll(mixed, 1, 1))
            to_left.append(pltpu.roll(mixed, LANES - 1, 1))
        out = []
        for j in range(cols):
            left = jnp.where(lane == 0, to_right[j - 1] if j else zero, to_right[j])
            right = jnp.where(lane == LANES - 1, to_left[j + 1] if j < cols - 1 else zero, to_left[j])
            out.append(sums[j] + (left + right))
        return out

    def rows_of(ref, c, i, many):
        return [[ref[c, i + k, j] for j in range(cols)] for k in range(many + 2)]

    def depth_step(d):
        take_halos(d)

        def screen(i, _):
            valid = row_valid(i)
            for j in range(cols):
                cosine, sine = cos_sin(angular * layer_thickness / vel[d, j, strided(i), :])
                sr, si, rr, ri = [nat[d, c, j, strided(i), :] for c in range(4)]
                cur_a[0, i + 1, j] = jnp.where(valid, sr * cosine + si * sine, 0.0)
                cur_a[1, i + 1, j] = jnp.where(valid, si * cosine - sr * sine, 0.0)
                cur_a[2, i + 1, j] = jnp.where(valid, rr * cosine - ri * sine, 0.0)
                cur_a[3, i + 1, j] = jnp.where(valid, ri * cosine + rr * sine, 0.0)
            return 0

        lax.fori_loop(0, count, screen, 0, unroll=2)
        wrap_rows(cur_a)

        def first(i, _):
            valid = row_valid(i)
            coefs = []
            for j in range(cols):
                speed = vel[d, j, strided(i), :]
                real = pade_second * (speed / (angular * grid_spacing)) ** 2
                imag = -pade_first * layer_thickness * speed / (2.0 * angular * grid_spacing**2)
                diag = 6.0 + 20.0 * real
                inverse = 1.0 / (diag * diag + 400.0 * imag * imag)
                couple_r = jnp.where(valid, 4.0 * (real * diag + 20.0 * imag * imag) * inverse, 0.0)
                couple_i = jnp.where(valid, 24.0 * imag * inverse, 0.0)
                coup[0, i, j] = couple_r
                coup[1, i, j] = couple_i
                six = jnp.where(valid, 6.0 * inverse, 0.0)
                coefs.append((real, imag, six * diag, 20.0 * six * imag, couple_r, couple_i))
            for field in range(2):
                r, m = 2 * field, 2 * field + 1
                near_r = quarter_stencil(*rows_of(cur_a, r, i, 1))
                near_i = quarter_stencil(*rows_of(cur_a, m, i, 1))
                for j in range(cols):
                    real, imag, over_r, over_i, couple_r, couple_i = coefs[j]
                    if field:
                        imag, over_i, couple_i = -imag, -over_i, -couple_i
                    u_r, u_i = cur_a[r, i + 1, j], cur_a[m, i + 1, j]
                    lap_r = (4.0 / 6.0) * near_r[j] - (20.0 / 6.0) * u_r
                    lap_i = (4.0 / 6.0) * near_i[j] - (20.0 / 6.0) * u_i
                    rhs_r = u_r - (real * lap_r + imag * lap_i)
                    rhs_i = u_i - (real * lap_i - imag * lap_r)
                    base_r = rhs_r * over_r + over_i * rhs_i
                    base_i = rhs_i * over_r - over_i * rhs_r
                    base_r = jnp.where(valid, base_r, 0.0)
                    base_i = jnp.where(valid, base_i, 0.0)
                    base[r, i, j] = base_r
                    base[m, i, j] = base_i
                    cur_b[r, i + 1, j] = base_r + (couple_r * near_r[j] - couple_i * near_i[j])
                    cur_b[m, i + 1, j] = base_i + (couple_r * near_i[j] + couple_i * near_r[j])
            return 0

        lax.fori_loop(0, count, first, 0)
        wrap_rows(cur_b)

        def update(ref, i, many, store):
            for field in range(2):
                r, m = 2 * field, 2 * field + 1
                lines_r, lines_i = rows_of(ref, r, i, many), rows_of(ref, m, i, many)
                for k in range(many):
                    near_r = quarter_stencil(*lines_r[k : k + 3])
                    near_i = quarter_stencil(*lines_i[k : k + 3])
                    for j in range(cols):
                        couple_r, couple_i = coup[0, i + k, j], coup[1, i + k, j]
                        cross_r, cross_i = couple_i * near_i[j], couple_i * near_r[j]
                        main_r = base[r, i + k, j] + couple_r * near_r[j]
                        main_i = base[m, i + k, j] + couple_r * near_i[j]
                        if field:
                            store(r, i + k, j, main_r + cross_r)
                            store(m, i + k, j, main_i - cross_i)
                        else:
                            store(r, i + k, j, main_r - cross_r)
                            store(m, i + k, j, main_i + cross_i)

        def over_rows(ref, store):
            def body(b, _):
                update(ref, b * BATCH, BATCH, store)
                return 0

            lax.fori_loop(0, count // BATCH, body, 0)

        def store_a(c, i, j, value):
            cur_a[c, i + 1, j] = value

        def store_b(c, i, j, value):
            cur_b[c, i + 1, j] = value

        def store_last(c, i, j, value):
            nat[d + 1, c, j, strided(i), :] = value

        def two_sweeps(_, carry):
            over_rows(cur_b, store_a)
            wrap_rows(cur_a)
            over_rows(cur_a, store_b)
            wrap_rows(cur_b)
            return carry

        lax.fori_loop(0, (SWEEPS - 2) // 2, two_sweeps, 0)
        over_rows(cur_b, store_last)

        @pl.when(d + 1 < STEPS)
        def _():
            send_halos(d + 1)

        for k in range(1, group):
            field_copy(d, k, member).start()
        top = pl.multiple_of(HALO + member * chunk, 8)

        def keep(c, _):
            recv[d, member, c] = nat[d + 1, c, :, pl.ds(top, chunk), :]
            return 0

        lax.fori_loop(0, 4, keep, 0)

    def shifted(blocks, move):
        if move == 0:
            return blocks
        if move > 0:
            rolled = [pltpu.roll(b, LANES - move, 1) for b in blocks] + [zero]
            inside = lane < LANES - move
            return [jnp.where(inside, rolled[j], rolled[j + 1]) for j in range(cols)]
        rolled = [zero] + [pltpu.roll(b, -move, 1) for b in blocks]
        inside = lane >= -move
        return [jnp.where(inside, rolled[j + 1], rolled[j]) for j in range(cols)]

    def image_step(d):
        for k in range(1, group):
            field_copy(d, k, (member + k) % group).wait_recv()

        def block(rb, _):
            top = pl.multiple_of(rb * 8, 8)
            for o in range(OFFS):
                h = o - OFFS // 2

                total = [None] * cols
                for q in range(group):
                    real = shifted([recv[d, q, 2, j, pl.ds(top, 8), :] for j in range(cols)], 2 * h)
                    imag = shifted([recv[d, q, 3, j, pl.ds(top, 8), :] for j in range(cols)], 2 * h)
                    for j in range(cols):
                        term = recv[d, q, 0, j, pl.ds(top, 8), :] * real[j] + recv[d, q, 1, j, pl.ds(top, 8), :] * imag[j]
                        total[j] = term if q == 0 else total[j] + term
                total = shifted(total, -h)
                for j in range(cols):
                    img[d, o, pl.ds(top, 8), pl.ds(j * LANES, LANES)] = total[j] * (1.0 / math.sqrt(n))
            return 0

        lax.fori_loop(0, chunk // 8, block, 0)
        for k in range(1, n):
            image_copy(d, k, me).start()
        place = pl.multiple_of(member * chunk, 8)
        for o in range(per_dev):
            part[d, my_group, o, pl.ds(place, chunk), :] = img[d, me * per_dev + o]

    def pipeline(d, _):
        @pl.when(d < STEPS)
        def _():
            depth_step(d)

        @pl.when(d > 0)
        def _():
            image_step(d - 1)

        return 0

    lax.fori_loop(0, STEPS + 1, pipeline, 0)

    def finish(d, _):
        for k in range(1, n):
            image_copy(d, k, (me + k) % n).wait_recv()

        def merge(b, _):
            top = pl.multiple_of(b * 8, 8)
            for o in range(per_dev):
                total = part[d, 0, o, pl.ds(top, 8), :]
                for gr in range(1, groups):
                    total = total + part[d, gr, o, pl.ds(top, 8), :]
                out_ref[d, o, pl.ds(top, 8), :] = total
            return 0

        lax.fori_loop(0, rows // 8, merge, 0)
        for k in range(1, group):
            field_copy(d, k, member).wait_send()
        for k in range(1, n):
            image_copy(d, k, me).wait_send()

        @pl.when(has_up)
        def _():
            halo_copy(d, 0).wait_send()

        @pl.when(has_down)
        def _():
            halo_copy(d, 1).wait_send()

        return 0

    lax.fori_loop(0, STEPS, finish, 0)

    @pl.when(has_up)
    def _():
        vel_copy(0).wait_send()

    @pl.when(has_down)
    def _():
        vel_copy(1).wait_send()


def on_device(n, tiles, wave, velocity):
    rows, width = velocity.shape[1:]
    cols = width // LANES
    ext = rows + 2 * HALO
    count = ext // 8
    group = min(4, n)
    chunk = rows // group
    per_dev = OFFS // n
    f32 = jnp.float32
    dma = pltpu.SemaphoreType.DMA
    return pl.pallas_call(
        functools.partial(kernel, n, tiles, group),
        out_shape=jax.ShapeDtypeStruct((STEPS, per_dev, rows, width), f32),
        in_specs=[pl.BlockSpec(memory_space=pltpu.VMEM)] * 2,
        out_specs=pl.BlockSpec(memory_space=pltpu.VMEM),
        scratch_shapes=[
            pltpu.VMEM((STEPS + 1, 4, cols, ext, LANES), f32),
            pltpu.VMEM((STEPS, 2, 4, cols, HALO, LANES), f32),
            pltpu.VMEM((STEPS, cols, ext, LANES), f32),
            pltpu.VMEM((4, count + 2, cols, 8, LANES), f32),
            pltpu.VMEM((4, count + 2, cols, 8, LANES), f32),
            pltpu.VMEM((4, count, cols, 8, LANES), f32),
            pltpu.VMEM((2, count, cols, 8, LANES), f32),
            pltpu.VMEM((STEPS, group, 4, cols, chunk, LANES), f32),
            pltpu.VMEM((STEPS, OFFS, chunk, width), f32),
            pltpu.VMEM((STEPS, n // group, per_dev, rows, width), f32),
            dma((2, 2)),
            dma((2, STEPS, 2)),
            dma((STEPS, group)),
            dma((STEPS, group)),
            dma((STEPS, n)),
            dma((STEPS, n)),
        ],
        compiler_params=pltpu.CompilerParams(
            collective_id=0, has_side_effects=True, vmem_limit_bytes=56 * 2**20
        ),
        name="migrate",
    )(wave, velocity)


def solution(mesh):
    placed = (P(None, None, "freq", "tile", None), P(None, "tile", None))
    return jax.shard_map(
        functools.partial(on_device, mesh.shape["freq"], mesh.shape["tile"]),
        mesh=mesh,
        in_specs=placed,
        out_specs=P(None, "freq", "tile", None),
        check_vma=False,
    )
```

```python
import functools
import math

import jax
import jax.numpy as jnp
from jax import lax
from jax.experimental import pallas as pl
from jax.experimental.pallas import tpu as pltpu
from jax.sharding import PartitionSpec as P

STEPS = 3
SWEEPS = 8
OFFS = 16
HALO = 8
LANES = 128
BATCH = 2

pade_first = 0.376393
pade_second = 0.478242
layer_thickness = 10.0
grid_spacing = 15.0
full_turn = 2.0 * math.pi
angle_mid = 1.2
MESH = pl.DeviceIdType.MESH


def cos_sin(angle):
    y = angle - angle_mid
    z = y * y
    sine = -1.0 / math.factorial(11)
    for power in (9, 7, 5, 3, 1):
        sine = sine * z + (-1.0) ** (power // 2) / math.factorial(power)
    sine = sine * y
    cosine = 1.0 / math.factorial(12)
    for power in (10, 8, 6, 4, 2, 0):
        cosine = cosine * z + (-1.0) ** (power // 2) / math.factorial(power)
    mid_cos, mid_sin = math.cos(angle_mid), math.sin(angle_mid)
    return cosine * mid_cos - sine * mid_sin, sine * mid_cos + cosine * mid_sin


def kernel(
    n, tiles, group, wave_ref, velocity_ref, out_ref, nat, halo, vel, cur_a, cur_b, base, coup, recv, img, part,
    vel_sems, halo_sems, field_send, field_recv, image_send, image_recv,
):
    rows, width = velocity_ref.shape[1:]
    cols = width // LANES
    ext = rows + 2 * HALO
    count = ext // 8
    chunk = rows // group
    groups = n // group
    per_dev = OFFS // n
    me = lax.axis_index("freq")
    tile = lax.axis_index("tile")
    my_group, member = me // group, me % group
    has_up, has_down = tile > 0, tile < tiles - 1

    lane = lax.broadcasted_iota(jnp.int32, (8, LANES), 1)
    sub = lax.broadcasted_iota(jnp.int32, (8, LANES), 0)
    angular = full_turn * (8.0 + 48.0 * jnp.full((8, LANES), me, jnp.int32).astype(jnp.float32) / n)
    zero = jnp.zeros((8, LANES), jnp.float32)

    def strided(i):
        return pl.ds(i, 8, stride=count)

    def row_valid(i):
        row = sub * count + (i - HALO + tile * rows)
        return (row >= 0) & (row < tiles * rows)

    def stage(k, _):
        top = pl.multiple_of(k * 8, 8)
        for j in range(cols):
            at = pl.ds(j * LANES, LANES)
            for c in range(4):
                nat[0, c, j, pl.ds(top + HALO, 8), :] = wave_ref[c // 2, c % 2, 0, pl.ds(top, 8), at]
            for d in range(STEPS):
                vel[d, j, pl.ds(top + HALO, 8), :] = velocity_ref[d, pl.ds(top, 8), at]
        return 0

    lax.fori_loop(0, rows // 8, stage, 0)

    barrier = pltpu.get_barrier_semaphore()
    for k in range(1, n):
        pl.semaphore_signal(barrier, inc=1, device_id={"freq": (me + k) % n}, device_id_type=MESH)

    @pl.when(has_up)
    def _():
        pl.semaphore_signal(barrier, inc=1, device_id={"tile": tile - 1}, device_id_type=MESH)

    @pl.when(has_down)
    def _():
        pl.semaphore_signal(barrier, inc=1, device_id={"tile": tile + 1}, device_id_type=MESH)

    near = (tile + tiles - 1) // tiles + (2 * tiles - 2 - tile) // tiles
    pl.semaphore_wait(barrier, n - 1 + near)

    def halo_copy(d, side):
        start = HALO if side == 0 else rows
        return pltpu.make_async_remote_copy(
            src_ref=nat.at[d, :, :, pl.ds(start, HALO), :],
            dst_ref=halo.at[d, side],
            send_sem=halo_sems.at[0, d, side],
            recv_sem=halo_sems.at[1, d, side],
            device_id={"tile": tile - 1 if side == 0 else tile + 1},
            device_id_type=MESH,
        )

    def vel_copy(side):
        start = HALO if side == 0 else rows
        land = rows + HALO if side == 0 else 0
        return pltpu.make_async_remote_copy(
            src_ref=vel.at[:, :, pl.ds(start, HALO), :],
            dst_ref=vel.at[:, :, pl.ds(land, HALO), :],
            send_sem=vel_sems.at[0, side],
            recv_sem=vel_sems.at[1, side],
            device_id={"tile": tile - 1 if side == 0 else tile + 1},
            device_id_type=MESH,
        )

    def field_copy(d, k, sender):
        peer = (member + k) % group
        return pltpu.make_async_remote_copy(
            src_ref=nat.at[d + 1, :, :, pl.ds(pl.multiple_of(HALO + peer * chunk, 8), chunk), :],
            dst_ref=recv.at[d, sender],
            send_sem=field_send.at[d, k],
            recv_sem=field_recv.at[d, sender],
            device_id={"freq": my_group * group + peer},
            device_id_type=MESH,
        )

    def image_copy(d, k, sender):
        peer = (me + k) % n
        top = pl.multiple_of((sender % group) * chunk, 8)
        return pltpu.make_async_remote_copy(
            src_ref=img.at[d, pl.ds(peer * per_dev, per_dev)],
            dst_ref=part.at[d, sender // group, :, pl.ds(top, chunk), :],
            send_sem=image_send.at[d, k],
            recv_sem=image_recv.at[d, sender],
            device_id={"freq": peer},
            device_id_type=MESH,
        )

    def send_halos(d):
        @pl.when(has_up)
        def _():
            halo_copy(d, 0).start()

        @pl.when(has_down)
        def _():
            halo_copy(d, 1).start()

    def take_halos(d):
        @pl.when(has_up)
        def _():
            halo_copy(d, 1).wait_recv()
            for c in range(4):
                for j in range(cols):
                    nat[d, c, j, 0:HALO, :] = halo[d, 1, c, j]

        @pl.when(has_down)
        def _():
            halo_copy(d, 0).wait_recv()
            for c in range(4):
                for j in range(cols):
                    nat[d, c, j, rows + HALO : rows + 2 * HALO, :] = halo[d, 0, c, j]

    @pl.when(has_up)
    def _():
        vel_copy(0).start()

    @pl.when(has_down)
    def _():
        vel_copy(1).start()

    send_halos(0)

    @pl.when(has_up)
    def _():
        vel_copy(1).wait_recv()

    @pl.when(has_down)
    def _():
        vel_copy(0).wait_recv()

    def wrap_rows(ref):
        for c in range(4):
            for j in range(cols):
                ref[c, 0, j] = pltpu.roll(ref[c, count, j], 1, 0)
                ref[c, count + 1, j] = pltpu.roll(ref[c, 1, j], 7, 0)

    def quarter_stencil(above, here, below):
        sums, to_right, to_left = [], [], []
        for j in range(cols):
            pair = above[j] + below[j]
            mixed = here[j] + 0.25 * pair
            sums.append(pair)
            to_right.append(pltpu.roll(mixed, 1, 1))
            to_left.append(pltpu.roll(mixed, LANES - 1, 1))
        out = []
        for j in range(cols):
            left = jnp.where(lane == 0, to_right[j - 1] if j else zero, to_right[j])
            right = jnp.where(lane == LANES - 1, to_left[j + 1] if j < cols - 1 else zero, to_left[j])
            out.append(sums[j] + (left + right))
        return out

    def rows_of(ref, c, i, many):
        return [[ref[c, i + k, j] for j in range(cols)] for k in range(many + 2)]

    def depth_step(d):
        take_halos(d)

        def screen(i, _):
            valid = row_valid(i)
            for j in range(cols):
                cosine, sine = cos_sin(angular * layer_thickness / vel[d, j, strided(i), :])
                sr, si, rr, ri = [nat[d, c, j, strided(i), :] for c in range(4)]
                cur_a[0, i + 1, j] = jnp.where(valid, sr * cosine + si * sine, 0.0)
                cur_a[1, i + 1, j] = jnp.where(valid, si * cosine - sr * sine, 0.0)
                cur_a[2, i + 1, j] = jnp.where(valid, rr * cosine - ri * sine, 0.0)
                cur_a[3, i + 1, j] = jnp.where(valid, ri * cosine + rr * sine, 0.0)
            return 0

        lax.fori_loop(0, count, screen, 0, unroll=2)
        wrap_rows(cur_a)

        def first(i, _):
            valid = row_valid(i)
            coefs = []
            for j in range(cols):
                speed = vel[d, j, strided(i), :]
                real = pade_second * (speed / (angular * grid_spacing)) ** 2
                imag = -pade_first * layer_thickness * speed / (2.0 * angular * grid_spacing**2)
                diag = 6.0 + 20.0 * real
                inverse = 1.0 / (diag * diag + 400.0 * imag * imag)
                couple_r = jnp.where(valid, 4.0 * (real * diag + 20.0 * imag * imag) * inverse, 0.0)
                couple_i = jnp.where(valid, 24.0 * imag * inverse, 0.0)
                coup[0, i, j] = couple_r
                coup[1, i, j] = couple_i
                six = jnp.where(valid, 6.0 * inverse, 0.0)
                coefs.append((real, imag, six * diag, 20.0 * six * imag, couple_r, couple_i))
            for field in range(2):
                r, m = 2 * field, 2 * field + 1
                near_r = quarter_stencil(*rows_of(cur_a, r, i, 1))
                near_i = quarter_stencil(*rows_of(cur_a, m, i, 1))
                for j in range(cols):
                    real, imag, over_r, over_i, couple_r, couple_i = coefs[j]
                    if field:
                        imag, over_i, couple_i = -imag, -over_i, -couple_i
                    u_r, u_i = cur_a[r, i + 1, j], cur_a[m, i + 1, j]
                    lap_r = (4.0 / 6.0) * near_r[j] - (20.0 / 6.0) * u_r
                    lap_i = (4.0 / 6.0) * near_i[j] - (20.0 / 6.0) * u_i
                    rhs_r = u_r - (real * lap_r + imag * lap_i)
                    rhs_i = u_i - (real * lap_i - imag * lap_r)
                    base_r = rhs_r * over_r + over_i * rhs_i
                    base_i = rhs_i * over_r - over_i * rhs_r
                    base_r = jnp.where(valid, base_r, 0.0)
                    base_i = jnp.where(valid, base_i, 0.0)
                    base[r, i, j] = base_r
                    base[m, i, j] = base_i
                    cur_b[r, i + 1, j] = base_r + (couple_r * near_r[j] - couple_i * near_i[j])
                    cur_b[m, i + 1, j] = base_i + (couple_r * near_i[j] + couple_i * near_r[j])
            return 0

        lax.fori_loop(0, count, first, 0)
        wrap_rows(cur_b)

        def update(ref, i, many, store):
            for field in range(2):
                r, m = 2 * field, 2 * field + 1
                lines_r, lines_i = rows_of(ref, r, i, many), rows_of(ref, m, i, many)
                for k in range(many):
                    near_r = quarter_stencil(*lines_r[k : k + 3])
                    near_i = quarter_stencil(*lines_i[k : k + 3])
                    for j in range(cols):
                        couple_r, couple_i = coup[0, i + k, j], coup[1, i + k, j]
                        cross_r, cross_i = couple_i * near_i[j], couple_i * near_r[j]
                        main_r = base[r, i + k, j] + couple_r * near_r[j]
                        main_i = base[m, i + k, j] + couple_r * near_i[j]
                        if field:
                            store(r, i + k, j, main_r + cross_r)
                            store(m, i + k, j, main_i - cross_i)
                        else:
                            store(r, i + k, j, main_r - cross_r)
                            store(m, i + k, j, main_i + cross_i)

        def over_rows(ref, store):
            def body(b, _):
                update(ref, b * BATCH, BATCH, store)
                return 0

            lax.fori_loop(0, count // BATCH, body, 0)

        def store_a(c, i, j, value):
            cur_a[c, i + 1, j] = value

        def store_b(c, i, j, value):
            cur_b[c, i + 1, j] = value

        def store_last(c, i, j, value):
            nat[d + 1, c, j, strided(i), :] = value

        def two_sweeps(_, carry):
            over_rows(cur_b, store_a)
            wrap_rows(cur_a)
            over_rows(cur_a, store_b)
            wrap_rows(cur_b)
            return carry

        lax.fori_loop(0, (SWEEPS - 2) // 2, two_sweeps, 0)

        @pl.when(d == 1)
        def _():
            image_step(0)

        over_rows(cur_b, store_last)

        @pl.when(d + 1 < STEPS)
        def _():
            send_halos(d + 1)

        for k in range(1, group):
            field_copy(d, k, member).start()
        top = pl.multiple_of(HALO + member * chunk, 8)

        def keep(c, _):
            recv[d, member, c] = nat[d + 1, c, :, pl.ds(top, chunk), :]
            return 0

        lax.fori_loop(0, 4, keep, 0)

    def shifted(blocks, move):
        if move == 0:
            return blocks
        if move > 0:
            rolled = [pltpu.roll(b, LANES - move, 1) for b in blocks] + [zero]
            inside = lane < LANES - move
            return [jnp.where(inside, rolled[j], rolled[j + 1]) for j in range(cols)]
        rolled = [zero] + [pltpu.roll(b, -move, 1) for b in blocks]
        inside = lane >= -move
        return [jnp.where(inside, rolled[j + 1], rolled[j]) for j in range(cols)]

    def image_step(d):
        for k in range(1, group):
            field_copy(d, k, (member + k) % group).wait_recv()

        def block(rb, _):
            top = pl.multiple_of(rb * 8, 8)
            for o in range(OFFS):
                h = o - OFFS // 2

                total = [None] * cols
                for q in range(group):
                    real = shifted([recv[d, q, 2, j, pl.ds(top, 8), :] for j in range(cols)], 2 * h)
                    imag = shifted([recv[d, q, 3, j, pl.ds(top, 8), :] for j in range(cols)], 2 * h)
                    for j in range(cols):
                        term = recv[d, q, 0, j, pl.ds(top, 8), :] * real[j] + recv[d, q, 1, j, pl.ds(top, 8), :] * imag[j]
                        total[j] = term if q == 0 else total[j] + term
                total = shifted(total, -h)
                for j in range(cols):
                    img[d, o, pl.ds(top, 8), pl.ds(j * LANES, LANES)] = total[j] * (1.0 / math.sqrt(n))
            return 0

        lax.fori_loop(0, chunk // 8, block, 0)
        for k in range(1, n):
            image_copy(d, k, me).start()
        place = pl.multiple_of(member * chunk, 8)
        for o in range(per_dev):
            part[d, my_group, o, pl.ds(place, chunk), :] = img[d, me * per_dev + o]

    def pipeline(d, _):
        @pl.when(d < STEPS)
        def _():
            depth_step(d)

        @pl.when(d > 1)
        def _():
            image_step(d - 1)

        return 0

    lax.fori_loop(0, STEPS + 1, pipeline, 0)

    def finish(d, _):
        for k in range(1, n):
            image_copy(d, k, (me + k) % n).wait_recv()

        def merge(b, _):
            top = pl.multiple_of(b * 8, 8)
            for o in range(per_dev):
                total = part[d, 0, o, pl.ds(top, 8), :]
                for gr in range(1, groups):
                    total = total + part[d, gr, o, pl.ds(top, 8), :]
                out_ref[d, o, pl.ds(top, 8), :] = total
            return 0

        lax.fori_loop(0, rows // 8, merge, 0)
        for k in range(1, group):
            field_copy(d, k, member).wait_send()
        for k in range(1, n):
            image_copy(d, k, me).wait_send()

        @pl.when(has_up)
        def _():
            halo_copy(d, 0).wait_send()

        @pl.when(has_down)
        def _():
            halo_copy(d, 1).wait_send()

        return 0

    lax.fori_loop(0, STEPS, finish, 0)

    @pl.when(has_up)
    def _():
        vel_copy(0).wait_send()

    @pl.when(has_down)
    def _():
        vel_copy(1).wait_send()


def on_device(n, tiles, wave, velocity):
    rows, width = velocity.shape[1:]
    cols = width // LANES
    ext = rows + 2 * HALO
    count = ext // 8
    group = min(4, n)
    chunk = rows // group
    per_dev = OFFS // n
    f32 = jnp.float32
    dma = pltpu.SemaphoreType.DMA
    return pl.pallas_call(
        functools.partial(kernel, n, tiles, group),
        out_shape=jax.ShapeDtypeStruct((STEPS, per_dev, rows, width), f32),
        in_specs=[pl.BlockSpec(memory_space=pltpu.VMEM)] * 2,
        out_specs=pl.BlockSpec(memory_space=pltpu.VMEM),
        scratch_shapes=[
            pltpu.VMEM((STEPS + 1, 4, cols, ext, LANES), f32),
            pltpu.VMEM((STEPS, 2, 4, cols, HALO, LANES), f32),
            pltpu.VMEM((STEPS, cols, ext, LANES), f32),
            pltpu.VMEM((4, count + 2, cols, 8, LANES), f32),
            pltpu.VMEM((4, count + 2, cols, 8, LANES), f32),
            pltpu.VMEM((4, count, cols, 8, LANES), f32),
            pltpu.VMEM((2, count, cols, 8, LANES), f32),
            pltpu.VMEM((STEPS, group, 4, cols, chunk, LANES), f32),
            pltpu.VMEM((STEPS, OFFS, chunk, width), f32),
            pltpu.VMEM((STEPS, n // group, per_dev, rows, width), f32),
            dma((2, 2)),
            dma((2, STEPS, 2)),
            dma((STEPS, group)),
            dma((STEPS, group)),
            dma((STEPS, n)),
            dma((STEPS, n)),
        ],
        compiler_params=pltpu.CompilerParams(
            collective_id=0, has_side_effects=True, vmem_limit_bytes=56 * 2**20
        ),
        name="migrate",
    )(wave, velocity)


def solution(mesh):
    placed = (P(None, None, "freq", "tile", None), P(None, "tile", None))
    return jax.shard_map(
        functools.partial(on_device, mesh.shape["freq"], mesh.shape["tile"]),
        mesh=mesh,
        in_specs=placed,
        out_specs=P(None, "freq", "tile", None),
        check_vma=False,
    )
```
